32 devices in a mesh: tm: 8 (over z, core), space: 4 (over y, x).
Axes of the slice: x: 2, y: 2, z: 4, core: 2. Of those that a mesh axis runs over, the one named last changes fastest.
Arguments:
- x_tokens: bfloat16 [8, 512, 6144], P('tm', 'space'), may hold values from -10 to 10
- win_rows: int32 [8, 256], P('tm'), may hold values from 0 to 511, as said below
- w_query: bfloat16 [6144, 3072], P(None, 'space'), may hold values from -0.19136639 to 0.19136639
- w_key: bfloat16 [6144, 3072], P(None, 'space'), may hold values from -0.19136639 to 0.19136639
- w_value: bfloat16 [6144, 3072], P(None, 'space'), may hold values from -0.078125 to 0.078125
- out_grad: bfloat16 [8, 256, 3072], P('tm', None, 'space'), may hold values from -6 to 6
Outputs:
- attended: bfloat16 [8, 256, 3072], P('tm', None, 'space')
- grad_query: float32 [6144, 3072], P('tm', 'space')
- grad_key: float32 [6144, 3072], P('tm', 'space')
- grad_value: float32 [6144, 3072], P('tm', 'space')
The draws below stay inside these ranges and needn't reach their ends.
Inputs may be any that keep to these rules, and one draw needn't show every extreme that they name: `win_rows`: each group's window holds 256 distinct rows; rows 0 and 511 are in every window.
All inputs are finite; a program needn't handle non-finite values.
Results may differ from the reference program's by a relative error of at most 0.015.
The reference program's roundings to bfloat16 on the way count: a program that leaves them out, or rounds other values in their place, can miss the bound.
Values may be sent and summed in bfloat16 or wider, within the bound.
No kernel may reach another device: no remote copies, remote signals or barrier semaphores. Data moves between devices by JAX's collectives and lax.ppermute only.
A program may use at most 256 MiB of HBM per device.

```python
import math
import jax
import jax.numpy as jnp
from jax import lax

D = 6144
H = 24
HD = 128
QW = 256
GROUPS = 8
TC = 512
HH = 3072


def draw_x_tokens(key, part):
    normals = jnp.clip(jax.random.normal(key, (GROUPS, TC, D), jnp.float32), -4.0, 4.0)
    return normals.astype(jnp.bfloat16)


def mixed_weight(key, own_tag):
    own_part = jnp.clip(jax.random.normal(jax.random.fold_in(key, own_tag), (D, H * HD), jnp.float32), -4.0, 4.0)
    return (2.0 * own_part * D ** (-0.5)).astype(jnp.bfloat16)


def draw_w_query(key, part):
    return mixed_weight(key, 12)


def draw_w_key(key, part):
    return mixed_weight(key, 13)


def draw_win_rows(key, part):
    group_keys = jax.random.split(key, GROUPS)

    def per_group(group_key):
        interior = 1 + jax.random.permutation(jax.random.fold_in(group_key, 1), TC - 2)[:QW - 2]
        window_rows = jnp.concatenate([jnp.array([0, TC - 1], jnp.int32), interior.astype(jnp.int32)])
        return jax.random.permutation(jax.random.fold_in(group_key, 2), window_rows)
    return jax.vmap(per_group)(group_keys).astype(jnp.int32)


def shard_levels(rng, dims, cuts, smallest, largest):
    level = 1.0
    for axis_at, shards_of in cuts:
        draws = jax.random.uniform(jax.random.fold_in(jax.random.fold_in(rng, 6), axis_at), (shards_of,), jnp.float32, smallest / len(cuts), largest / len(cuts))
        level = level * jnp.repeat(jnp.exp(draws), dims[axis_at] // shards_of).reshape((-1,) + (1,) * (len(dims) - 1 - axis_at))
    return level


def gaussian(rng, extent, deviation, bound, shards=(), dtype=jnp.bfloat16):
    values = jax.random.normal(rng, extent, jnp.float32) * deviation
    if len(shards) > 0:
        values = shard_levels(rng, extent, shards, -0.22, 0.18) * values
    return jnp.clip(values, min=-bound, max=bound).astype(dtype)


def setup_inputs(seed: int = 0) -> dict:
    key_of = jax.random.split(jax.random.key(seed), 7)
    x_tokens = draw_x_tokens(jax.random.fold_in(key_of[6], 71), 0)
    win_rows = draw_win_rows(jax.random.fold_in(key_of[6], 71), 0)
    w_query = draw_w_query(jax.random.fold_in(key_of[6], 71), 0)
    w_key = draw_w_key(jax.random.fold_in(key_of[6], 71), 0)
    w_value = gaussian(key_of[4], (D, HH), D ** -0.5, 0.078125, ((1, 4),))
    out_grad = gaussian(key_of[5], (GROUPS, QW, HH), 1.0, 6.0, ((0, 8), (2, 4)))
    return dict(x_tokens=x_tokens, win_rows=win_rows, w_query=w_query, w_key=w_key, w_value=w_value, out_grad=out_grad)


def attend(query_rows, key_rows, value_rows, grad_rows, allowed):
    scaling = 1.0 / math.sqrt(HD)
    query_heads = query_rows.reshape(QW, H, HD).astype(jnp.float32)
    key_heads = key_rows.reshape(-1, H, HD).astype(jnp.float32)
    value_heads = value_rows.reshape(-1, H, HD).astype(jnp.float32)
    grad_heads = grad_rows.reshape(QW, H, HD).astype(jnp.float32)
    scores = jnp.einsum('qhd,khd->hqk', query_heads, key_heads) * scaling
    scores = jnp.where(allowed[None, None, :], scores, -jnp.inf)
    row_max = lax.optimization_barrier(jnp.max(scores, axis=-1, keepdims=True))
    log_total = row_max + jnp.log(lax.optimization_barrier(jnp.sum(jnp.exp(scores - row_max), axis=-1, keepdims=True)))
    probabilities = jnp.exp(scores - log_total)
    prob_rounded = lax.optimization_barrier(probabilities.astype(jnp.bfloat16)).astype(jnp.float32)
    attended = jnp.einsum('hqk,khd->qhd', prob_rounded, value_heads).astype(jnp.bfloat16).reshape(QW, HH)
    prob_grads = jnp.einsum('qhd,khd->hqk', grad_heads, value_heads)
    row_inner = lax.optimization_barrier(jnp.sum(probabilities * prob_grads, axis=-1, keepdims=True))
    score_grads = probabilities * (prob_grads - row_inner) * scaling
    score_grads = lax.optimization_barrier(score_grads.astype(jnp.bfloat16)).astype(jnp.float32)
    query_grads = jnp.einsum('hqk,khd->qhd', score_grads, key_heads).astype(jnp.bfloat16).reshape(QW, HH)
    key_parts = jnp.einsum('hqk,qhd->khd', score_grads, query_heads).reshape(-1, HH)
    value_parts = jnp.einsum('hqk,qhd->khd', prob_rounded, grad_heads).reshape(-1, HH)
    return (attended, query_grads, key_parts, value_parts)

def reference(x_tokens, win_rows, w_query, w_key, w_value, out_grad):

    def project(group_x):
        key_rows = jnp.dot(group_x, w_key, preferred_element_type=jnp.float32).astype(jnp.bfloat16)
        value_rows = jnp.dot(group_x, w_value, preferred_element_type=jnp.float32).astype(jnp.bfloat16)
        return (key_rows, value_rows)
    all_keys, all_values = lax.map(project, x_tokens)

    def make_query(inputs):
        group_x, window_rows = inputs
        return jnp.dot(group_x[window_rows], w_query, preferred_element_type=jnp.float32).astype(jnp.bfloat16)
    queries = lax.map(make_query, (x_tokens, win_rows))
    zero_keys = jnp.zeros_like(all_keys[:1])
    keys_one = jnp.concatenate([zero_keys, all_keys[:-1]], axis=0)
    keys_two = jnp.concatenate([zero_keys, zero_keys, all_keys[:-2]], axis=0)[:GROUPS]
    values_one = jnp.concatenate([zero_keys, all_values[:-1]], axis=0)
    values_two = jnp.concatenate([zero_keys, zero_keys, all_values[:-2]], axis=0)[:GROUPS]
    key_block = jnp.arange(3 * TC) // TC

    def per_group(inputs):
        group_index, query_rows, key_far, key_near, key_own, value_far, value_near, value_own, grad_rows = inputs
        key_rows = jnp.concatenate([key_far, key_near, key_own], axis=0)
        value_rows = jnp.concatenate([value_far, value_near, value_own], axis=0)
        allowed = (key_block == 2) | (key_block == 1) & (group_index >= 1) | (key_block == 0) & (group_index >= 2)
        return attend(query_rows, key_rows, value_rows, grad_rows, allowed)
    group_ids = jnp.arange(GROUPS).astype(jnp.int32)
    attended, query_grads, key_parts, value_parts = lax.map(per_group, (group_ids, queries, keys_two, keys_one, all_keys, values_two, values_one, all_values, out_grad))
    zero_block = jnp.zeros((1, TC, HH), jnp.float32)

    def combine(parts):
        own_block = parts[:, 2 * TC:]
        near_block = jnp.concatenate([parts[1:, TC:2 * TC], zero_block], axis=0)
        far_block = jnp.concatenate([parts[2:, :TC], zero_block, zero_block], axis=0)[:GROUPS]
        return (own_block + near_block + far_block).astype(jnp.bfloat16)
    key_grad = combine(key_parts)
    value_grad = combine(value_parts)

    def rounded_term(left, right):
        term = jnp.dot(left.T, right, preferred_element_type=jnp.float32)
        return lax.optimization_barrier(term.astype(jnp.bfloat16)).astype(jnp.float32)

    def accumulate(carry, inputs):
        group_x, window_rows, query_part, key_part, value_part = inputs
        return ((carry[0] + rounded_term(group_x[window_rows], query_part), carry[1] + rounded_term(group_x, key_part), carry[2] + rounded_term(group_x, value_part)), None)
    zero_grad = jnp.zeros((D, HH), jnp.float32)
    totals, unused = lax.scan(accumulate, (zero_grad, zero_grad, zero_grad), (x_tokens, win_rows, query_grads, key_grad, value_grad))
    return (attended, totals[0], totals[1], totals[2])
```

```python
import functools
import math

import jax
import jax.numpy as jnp
from jax import lax
from jax.experimental import pallas as pl
from jax.experimental.pallas import tpu as pltpu
from jax.sharding import PartitionSpec as P

HD = 128
F32 = jnp.float32
BF16 = jnp.bfloat16
SCALE = 1.0 / math.sqrt(HD)
ABSENT = -1e30


def move(block, axis, route):
    return lax.ppermute(block, axis, route)


def shifted(block, axis, distance, first=0, last=None):
    size = lax.axis_size(axis)
    last = size if last is None else last
    route = [(i, i + distance) for i in range(first, last) if 0 <= i + distance < size]
    return move(block, axis, route)


def flipped(block, axis, bits, members=None):
    size = lax.axis_size(axis)
    members = range(size) if members is None else members
    return move(block, axis, [(i, i ^ bits) for i in members])


def doubled(own, axis):
    blocks, bit = [own], 1
    while bit < lax.axis_size(axis):
        blocks += [flipped(block, axis, bit) for block in blocks]
        bit *= 2
    return blocks


def nt(a, b):
    return lax.dot_general(a, b, (((1,), (1,)), ((), ())), preferred_element_type=F32)


def nn(a, b):
    return jnp.dot(a, b, preferred_element_type=F32)


def stats_kernel(q0, q1, q2, g0, g1, g2, k_ref, v_ref, stat_ref, o0, o1, o2):
    k, v = k_ref[...], v_ref[...]
    vt = v.T
    for b, (q, g, o) in enumerate(((q0, g0, o0), (q1, g1, o1), (q2, g2, o2))):
        s = nt(k, q[...]) * SCALE
        top = jnp.max(s, axis=0, keepdims=True)
        p = jnp.exp(s - top)
        total = jnp.sum(p, axis=0, keepdims=True)
        inner = jnp.sum(p * nt(v, g[...]), axis=0, keepdims=True)
        stat_ref[0, b : b + 1, :] = top + jnp.log(total)
        stat_ref[0, 3 + b : 4 + b, :] = inner / total
        o[...] = (nn(vt, p.astype(BF16)) / total).astype(o.dtype)


def attention_stats(q, g, keys, values):
    group_len, width = keys.shape
    rows = q[0].shape[0]
    heads = width // HD
    q_spec = pl.BlockSpec((rows, HD), lambda h: (0, h))
    k_spec = pl.BlockSpec((group_len, HD), lambda h: (0, h))
    o_spec = pl.BlockSpec((HD, rows), lambda h: (h, 0))
    flops = heads * 9 * 2 * rows * group_len * HD
    return pl.pallas_call(
        stats_kernel,
        grid=(heads,),
        in_specs=[q_spec] * 6 + [k_spec] * 2,
        out_specs=[pl.BlockSpec((1, 6, rows), lambda h: (h, 0, 0))] + [o_spec] * 3,
        out_shape=[jax.ShapeDtypeStruct((heads, 6, rows), F32)]
        + [jax.ShapeDtypeStruct((width, rows), dt) for dt in (F32, BF16, BF16)],
        cost_estimate=pl.CostEstimate(flops=flops, bytes_accessed=8 * width * group_len, transcendentals=0),
        name="attn_stats",
    )(*q, *g, keys, values)


def combine(parts):
    top = functools.reduce(jnp.maximum, [lse for lse, _ in parts])
    weights = [jnp.exp(lse - top) for lse, _ in parts]
    total = sum(weights)
    inner = sum(w * d for w, (_, d) in zip(weights, parts)) / total
    return top + jnp.log(total), inner


def present(ref, entry, flag):
    lse = jnp.where(flag, ref[0, entry : entry + 1, :], ABSENT)
    return lse, ref[0, 3 + entry : 4 + entry, :]


def grads_kernel(
    j_ref, q0, q1, q2, g0, g1, g2, k_ref, v_ref, own, behind1, behind2, ahead1, ahead2, kv_ref, d0, d1, d2
):
    j = j_ref[0]
    yes = j >= 0
    k, v = k_ref[...], v_ref[...]
    kt = k.T
    sources = (
        ((own, 0, yes), (behind1, 1, j >= 1), (behind2, 2, j >= 2)),
        ((ahead1, 0, yes), (own, 1, yes), (behind1, 2, j >= 1)),
        ((ahead2, 0, yes), (ahead1, 1, yes), (own, 2, yes)),
    )
    dk = dv = None
    for (q, g, d), source in zip(((q0, g0, d0), (q1, g1, d1), (q2, g2, d2)), sources):
        lse, inner = combine([present(*s) for s in source])
        queries, cotangent = q[...], g[...]
        p = jnp.exp(nt(k, queries) * SCALE - lse)
        ds = (p * (nt(v, cotangent) - inner) * SCALE).astype(BF16)
        dv_part = nn(p.astype(BF16), cotangent)
        dk_part = nn(ds, queries)
        dk = dk_part if dk is None else dk + dk_part
        dv = dv_part if dv is None else dv + dv_part
        d[...] = nn(kt, ds).T.astype(d.dtype)
    kv_ref[0] = dk.astype(BF16)
    kv_ref[1] = dv.astype(BF16)


def attention_grads(j, q, g, keys, values, stats):
    group_len, width = keys.shape
    rows = q[0].shape[0]
    heads = width // HD
    q_spec = pl.BlockSpec((rows, HD), lambda h, s: (0, h))
    k_spec = pl.BlockSpec((group_len, HD), lambda h, s: (0, h))
    s_spec = pl.BlockSpec((1, 6, rows), lambda h, s: (h, 0, 0))
    flops = heads * 15 * 2 * rows * group_len * HD
    return pl.pallas_call(
        grads_kernel,
        grid_spec=pltpu.PrefetchScalarGridSpec(
            num_scalar_prefetch=1,
            grid=(heads,),
            in_specs=[q_spec] * 6 + [k_spec] * 2 + [s_spec] * 5,
            out_specs=[pl.BlockSpec((2, group_len, HD), lambda h, s: (0, 0, h))] + [q_spec] * 3,
        ),
        out_shape=[jax.ShapeDtypeStruct((2, group_len, width), BF16)]
        + [jax.ShapeDtypeStruct((rows, width), dt) for dt in (F32, BF16, BF16)],
        cost_estimate=pl.CostEstimate(flops=flops, bytes_accessed=12 * width * group_len, transcendentals=0),
        name="attn_grads",
    )(j, *q, *g, keys, values, *stats)


def output_kernel(j_ref, o0, o1, o2, own, behind1, behind2, out_ref):
    j = j_ref[0]
    parts = [present(own, 0, j >= 0), present(behind1, 1, j >= 1), present(behind2, 2, j >= 2)]
    lse, _ = combine(parts)
    total = None
    for o, (part, _) in zip((o0, o1, o2), parts):
        term = o[...].astype(F32) * jnp.exp(part - lse)
        total = term if total is None else total + term
    out_ref[...] = total.T.astype(BF16)


def attention_output(j, o, stats):
    width, rows = o[0].shape
    heads = width // HD
    o_spec = pl.BlockSpec((HD, rows), lambda h, s: (h, 0))
    s_spec = pl.BlockSpec((1, 6, rows), lambda h, s: (h, 0, 0))
    return pl.pallas_call(
        output_kernel,
        grid_spec=pltpu.PrefetchScalarGridSpec(
            num_scalar_prefetch=1,
            grid=(heads,),
            in_specs=[o_spec] * 3 + [s_spec] * 3,
            out_specs=pl.BlockSpec((rows, HD), lambda h, s: (0, h)),
        ),
        out_shape=jax.ShapeDtypeStruct((rows, width), BF16),
        cost_estimate=pl.CostEstimate(flops=8 * width * rows, bytes_accessed=10 * width * rows, transcendentals=0),
        name="attn_output",
    )(j, *o, *stats)


def turn_kernel(pos_ref, *refs):
    pieces, (xt_ref, wt_ref) = refs[:-2], refs[-2:]
    chunk = pieces[0].shape[1]
    for i, piece in enumerate(pieces):
        xt_ref[0, :, i * chunk : (i + 1) * chunk] = piece[0].T
    group_len = len(pieces) * chunk
    rows = pos_ref.shape[2]
    token = lax.broadcasted_iota(jnp.int32, (group_len, rows), 0)
    pick = jnp.where(token == pos_ref[0], 1.0, 0.0).astype(BF16)
    wt_ref[0] = nn(xt_ref[0], pick).astype(BF16)


def turn(positions, pieces):
    groups, chunk, depth = pieces[0].shape
    group_len = len(pieces) * chunk
    rows = positions.shape[2]
    p_spec = pl.BlockSpec((1, chunk, depth), lambda c: (c, 0, 0))
    return pl.pallas_call(
        turn_kernel,
        grid=(groups,),
        in_specs=[pl.BlockSpec((1, 1, rows), lambda c: (c, 0, 0))] + [p_spec] * len(pieces),
        out_specs=[
            pl.BlockSpec((1, depth, group_len), lambda c: (c, 0, 0)),
            pl.BlockSpec((1, depth, rows), lambda c: (c, 0, 0)),
        ],
        out_shape=[
            jax.ShapeDtypeStruct((groups, depth, group_len), BF16),
            jax.ShapeDtypeStruct((groups, depth, rows), BF16),
        ],
        cost_estimate=pl.CostEstimate(
            flops=groups * 2 * group_len * depth * rows, bytes_accessed=groups * depth * group_len * 5, transcendentals=0
        ),
        name="turn_tokens",
    )(positions, *pieces)


def fold_kernel(pairs, select, first, idx_ref, *refs):
    xts, gs = refs[:pairs], refs[pairs : pairs + len(select)]
    rest = refs[pairs + len(select) :]
    acc = None if first else rest[0][0]
    out = rest[-1]
    at = 0
    for i in range(pairs):
        g = gs[at][0]
        if select[at] is not None:
            g = jnp.where(idx_ref[pairs] == 1, g, gs[at + 1][0])
            at += 1
        at += 1
        term = nn(xts[i][0], g)
        acc = term if acc is None else acc + term
    out[0] = acc


def fold(xt, sources, groups, use_first, acc):
    pairs = len(sources)
    flat, select = [], []
    for source in sources:
        if isinstance(source, tuple):
            flat += list(source)
            select += [True, True]
        else:
            flat.append(source)
            select.append(None)
    kinds, tokens, width = flat[0].shape
    depth = xt.shape[1]
    x_specs = [
        pl.BlockSpec((1, depth, tokens), functools.partial(lambda i, n, s: (s[i], 0, 0), i)) for i in range(pairs)
    ]
    g_spec = pl.BlockSpec((1, tokens, width), lambda n, s: (n, 0, 0))
    a_spec = pl.BlockSpec((1, depth, width), lambda n, s: (n, 0, 0))
    first = acc is None
    index = jnp.stack(list(groups) + [use_first]).astype(jnp.int32)
    extra = [] if first else [acc]
    return pl.pallas_call(
        functools.partial(fold_kernel, pairs, tuple(select), first),
        grid_spec=pltpu.PrefetchScalarGridSpec(
            num_scalar_prefetch=1,
            grid=(kinds,),
            in_specs=x_specs + [g_spec] * len(flat) + [a_spec] * len(extra),
            out_specs=a_spec,
        ),
        out_shape=jax.ShapeDtypeStruct((kinds, depth, width), F32),
        input_output_aliases={} if first else {1 + pairs + len(flat): 0},
        cost_estimate=pl.CostEstimate(
            flops=kinds * pairs * 2 * depth * tokens * width,
            bytes_accessed=kinds * (pairs * 2 * tokens * (depth + width) + 8 * depth * width),
            transcendentals=0,
        ),
        name="fold",
    )(index, *([xt] * pairs), *flat, *extra)


def spread(own, xt, j, acc=None):
    size = lax.axis_size("tm")
    chips = size // 2
    chip, core = j // 2, j % 2
    mine = lambda c: 2 * jnp.clip(c, 0, chips - 1) + core
    other = lambda c: 2 * jnp.clip(c, 0, chips - 1) + 1 - core
    partner = flipped(own, "tm", 1)
    right = left = own
    arrivals = []
    for step in range(1, chips):
        right = shifted(right, "tm", 2, first=2 * (step - 1))
        left = shifted(left, "tm", -2, last=size - 2 * (step - 1))
        right_other = flipped(right, "tm", 1, range(2 * step, size))
        left_other = flipped(left, "tm", 1, range(0, size - 2 * step))
        arrivals.append((step, right, right_other, left, left_other))
    yes = jnp.int32(1)
    acc = fold(xt, [own, partner], [mine(chip), other(chip)], yes, acc)
    for step, right, right_other, left, left_other in arrivals:
        if 2 * step >= chips:
            from_left = chip >= step
            source = jnp.where(from_left, chip - step, chip + step)
            acc = fold(
                xt,
                [(right, left), (right_other, left_other)],
                [mine(source), other(source)],
                from_left.astype(jnp.int32),
                acc,
            )
        else:
            acc = fold(
                xt,
                [right, right_other, left, left_other],
                [mine(chip - step), other(chip - step), mine(chip + step), other(chip + step)],
                yes,
                acc,
            )
    return acc


def project(tokens, weight):
    return nn(tokens, weight).astype(BF16)


def on_device(x_tokens, win_rows, w_query, w_key, w_value, out_grad):
    j = lax.axis_index("tm")
    s = lax.axis_index("space")
    groups = lax.axis_size("tm")
    own = x_tokens[0]
    chunk, model = own.shape
    half = chunk // 2
    depth = model // groups

    if lax.axis_size("space") == 4:
        upper, lower = own[:half], own[half:]
        x_upper = flipped(upper, "space", 1)
        y_lower = flipped(lower, "space", 2)
        x_lower = flipped(lower, "space", 1)
        y_upper = flipped(upper, "space", 2)
        far_upper = flipped(x_upper, "space", 2)
        far_lower = flipped(y_lower, "space", 1)
        arrived = [
            own,
            jnp.concatenate([x_upper, x_lower, y_upper, y_lower], axis=0),
            jnp.concatenate([far_upper, far_lower], axis=0),
        ]
    else:
        arrived = [jnp.concatenate(doubled(own, "space"), axis=0)]
    group_len = chunk * lax.axis_size("space")

    slab = lax.all_to_all(own, "tm", 1, 0, tiled=True).reshape(groups, chunk, depth)
    cotangent = out_grad[0]
    g = [cotangent, shifted(cotangent, "tm", -1), shifted(cotangent, "tm", -2)]
    rows = win_rows.shape[1]
    windows = lax.all_to_all(jnp.broadcast_to(win_rows, (groups, rows)), "tm", 0, 0)
    slabs = doubled(slab, "space")

    def placed(r):
        return ((r // chunk) ^ s) * chunk + r % chunk

    def projected(weight):
        return jnp.concatenate([project(t, weight) for t in arrived], axis=0)

    token = lax.broadcasted_iota(jnp.int32, (group_len, rows), 0)
    pick = (token == placed(win_rows)).astype(BF16)
    query = lax.dot_general(
        pick, projected(w_query), (((0,), (0,)), ((), ())), preferred_element_type=F32
    ).astype(BF16)
    q = [query, shifted(query, "tm", -1), shifted(query, "tm", -2)]
    keys = projected(w_key)
    values = projected(w_value)

    stats, o0, o1, o2 = attention_stats(q, g, keys, values)
    behind1, behind2 = shifted(stats, "tm", 1), shifted(stats, "tm", 2)
    ahead1, ahead2 = shifted(stats, "tm", -1), shifted(stats, "tm", -2)
    o1 = shifted(o1, "tm", 1)
    o2 = shifted(o2, "tm", 2)
    j_arr = j.astype(jnp.int32).reshape(1)
    kv_grad, d0, d1, d2 = attention_grads(
        j_arr, q, g, keys, values, [stats, behind1, behind2, ahead1, ahead2]
    )
    q_grad = (d0 + shifted(d1, "tm", 1).astype(F32) + shifted(d2, "tm", 2).astype(F32)).astype(BF16)
    attended = attention_output(j_arr, [o0, o1, o2], [stats, behind1, behind2])

    xt, wt = turn(placed(windows)[:, None, :], slabs)
    kv = spread(kv_grad, xt, j)
    qg = spread(q_grad[None], wt, j)
    return attended[None], qg[0], kv[0], kv[1]


def solution(mesh):
    in_specs = (
        P("tm", "space", None),
        P("tm", None),
        P(None, "space"),
        P(None, "space"),
        P(None, "space"),
        P("tm", None, "space"),
    )
    out_specs = (P("tm", None, "space"), P("tm", "space"), P("tm", "space"), P("tm", "space"))
    return jax.shard_map(
        on_device, mesh=mesh, in_specs=in_specs, out_specs=out_specs, check_vma=False
    )
```
